768 devices in a mesh: ctx: 192 (over y, z_lo, x, core), head: 4 (over z_hi).
Axes of the slice: x: 4, y: 8, z: 12 (z_hi: 4, z_lo: 3; z = z_hi * 3 + z_lo), core: 2. Of those that a mesh axis runs over, the one named last changes fastest.
Arguments:
- patches: bfloat16 [49152, 2560], P('ctx', 'head'), may hold values from -120 to 120
- merge_index: int32 [192, 2], P('ctx'), may hold values from 0 to 383, as said below
- merge_vals: bfloat16 [192, 2, 128, 128], P('ctx'), may hold values from -0.375 to 0.375
- merger_weight: bfloat16 [2560, 4096], P('head'), may hold values from -0.125 to 0.125
- proj_weight: bfloat16 [4096, 3072], P(None, 'head'), may hold values from -0.09375 to 0.09375
- frame_ids: int32 [24576], replicated, may hold values from 0 to 575, as said below
Outputs:
- attended: bfloat16 [24576, 2048], P('ctx', 'head')
The draws below stay inside these ranges and needn't reach their ends.
Inputs may be any that keep to these rules, and one draw needn't show every extreme that they name: `merge_index`: the two entries of output block b are two different input blocks out of 2b - 1, 2b and 2b + 1, in rising order; never 2b - 1 when b is the first block of a video; always 2b - 1 when b is the first block of a slab (1 output blocks a slab) that is not the first of a video; the last output block always takes block 2b + 1. `frame_ids`: frame ids never fall along the tokens and frames never cross slabs: every slab of 128 tokens holds 3 frames, the first of 1 to 63 tokens, then frames of 64 tokens, the last one shorter.
All inputs are finite; a program needn't handle non-finite values.
Results may differ from the reference program's by a relative error of at most 0.033.
Values may be sent and summed in bfloat16 or wider, within the bound.
No kernel may reach another device: no remote copies, remote signals or barrier semaphores. Data moves between devices by JAX's collectives and lax.ppermute only.
A program may use at most 128 MiB of HBM per device.

```python
import math
import jax
import jax.numpy as jnp
from jax import lax

C = 2560
HID = 4096
HD = 128
QPK = 4
BLK = 128
KB = 2
FRAME_MOST = 64
TOK_DEV = 128
FIRST_DEVS = 120
TOKENS = 24576
ROWS = 49152
OUT_BLOCKS = 192
KVH = 4
FIRST_TOK = 15360


def draw_patches(key, part):
    noise_key = jax.random.fold_in(key, 0)
    values = jnp.clip(jax.random.normal(noise_key, (ROWS, C), jnp.float32), -6.0, 6.0)
    return values.astype(jnp.bfloat16)


def draw_merge_index(key, part):
    first_key, slab_key = jax.random.split(key)
    blocks = jnp.arange(OUT_BLOCKS, dtype=jnp.int32)
    slab_blocks = TOK_DEV // BLK
    dropped = jax.random.randint(first_key, (OUT_BLOCKS,), 0, 3, dtype=jnp.int32)
    slab_first = blocks % slab_blocks == 0
    video_first = (blocks == 0) | (blocks == FIRST_DEVS * slab_blocks)
    forced = 1 + jax.random.randint(slab_key, (OUT_BLOCKS,), 0, 2, dtype=jnp.int32)
    dropped = jnp.where(slab_first, forced, dropped)
    dropped = jnp.where(video_first, 0, dropped)
    dropped = jnp.where(blocks == OUT_BLOCKS - 1, jnp.minimum(dropped, 1), dropped)
    lower_block = jnp.where(dropped == 0, 2 * blocks, 2 * blocks - 1)
    upper_block = jnp.where(dropped == 2, 2 * blocks, 2 * blocks + 1)
    return jnp.stack([lower_block, upper_block], axis=1).astype(jnp.int32)


def draw_frame_ids(key, part):
    slabs = TOKENS // TOK_DEV
    offsets = jax.random.randint(key, (slabs, 1), 1, FRAME_MOST, dtype=jnp.int32)
    local_row = jnp.arange(TOK_DEV, dtype=jnp.int32)[None, :]
    local_frame = jnp.where(local_row < offsets, 0, 1 + (local_row - offsets) // FRAME_MOST)
    slab_number = jnp.arange(slabs, dtype=jnp.int32)[:, None]
    frames = slab_number * (TOK_DEV // FRAME_MOST + 1) + local_frame
    return frames.reshape(TOKENS).astype(jnp.int32)


def shard_levels(key, shape, pieces, least, high):
    gain = 1.0
    for axis_at, blocks in pieces:
        heights = jax.random.uniform(jax.random.fold_in(jax.random.fold_in(key, 6), axis_at), (blocks,), jnp.float32, least / len(pieces), high / len(pieces))
        gain = gain * jnp.repeat(jnp.exp(heights), shape[axis_at] // blocks).reshape((-1,) + (1,) * (len(shape) - 1 - axis_at))
    return gain


def normal_values(key, extent, scale, limit, pieces=(), kind=jnp.bfloat16):
    drawn = jax.random.normal(key, extent, jnp.float32) * scale
    if len(pieces) > 0:
        drawn = shard_levels(key, extent, pieces, -0.22, 0.18) * drawn
    return jnp.clip(drawn, min=-limit, max=limit).astype(kind)


def setup_inputs(seed: int = 0) -> dict:
    splits = jax.random.split(jax.random.key(seed), 7)
    patches = draw_patches(jax.random.fold_in(splits[6], 71), 0)
    merge_index = draw_merge_index(jax.random.fold_in(splits[6], 71), 0)
    merge_vals = normal_values(splits[2], (OUT_BLOCKS, KB, BLK, BLK), (KB * BLK) ** -0.5, 0.375, ((0, 192),))
    merger_weight = normal_values(splits[3], (C, HID), C ** -0.5, 0.125, ((0, 4),))
    proj_weight = normal_values(splits[4], (HID, KVH * (QPK + 2) * HD), HID ** -0.5, 0.09375, ((1, 4),))
    frame_ids = draw_frame_ids(jax.random.fold_in(splits[6], 71), 0)
    return {"patches": patches, "merge_index": merge_index, "merge_vals": merge_vals, "merger_weight": merger_weight, "proj_weight": proj_weight, "frame_ids": frame_ids}


def reference(patches, merge_index, merge_vals, merger_weight, proj_weight, frame_ids):
    patch_blocks = patches.reshape(2 * OUT_BLOCKS, BLK, C)

    def merge_block(operands):
        block_list, block_vals = operands
        picked = jnp.take(patch_blocks, block_list.astype(jnp.int32), axis=0).astype(jnp.float32)
        summed = jnp.einsum('jrs,jsc->rc', block_vals.astype(jnp.float32), picked)
        return summed.astype(jnp.bfloat16)
    merged = lax.map(merge_block, (merge_index, merge_vals)).reshape(TOKENS, C)
    hidden = jnp.dot(merged, merger_weight, preferred_element_type=jnp.float32)
    mean_square = lax.optimization_barrier(jnp.mean(hidden * hidden, axis=-1, keepdims=True))
    normed = (hidden * lax.rsqrt(mean_square + 1e-06)).astype(jnp.bfloat16)
    projected = jnp.dot(normed, proj_weight, preferred_element_type=jnp.float32)
    projected = projected.reshape(TOKENS, KVH, QPK + 2, HD)
    queries = projected[:, :, :QPK].astype(jnp.bfloat16)
    keys = projected[:, :, QPK].astype(jnp.bfloat16)
    values = projected[:, :, QPK + 1].astype(jnp.bfloat16)
    query_rows = math.gcd(FIRST_TOK, 256)
    key_span = max(FIRST_TOK, TOKENS - FIRST_TOK)
    score_scale = 1.0 / math.sqrt(HD)

    def attend_block(block_number):
        first_row = (block_number * query_rows).astype(jnp.int32)
        query_video = (first_row >= FIRST_TOK).astype(jnp.int32)
        key_start = jnp.where(query_video == 1, TOKENS - key_span, 0).astype(jnp.int32)
        block_queries = lax.dynamic_slice_in_dim(queries, first_row, query_rows).astype(jnp.float32)
        video_keys = lax.dynamic_slice_in_dim(keys, key_start, key_span).astype(jnp.float32)
        video_values = lax.dynamic_slice_in_dim(values, key_start, key_span).astype(jnp.float32)
        query_frames = lax.dynamic_slice_in_dim(frame_ids, first_row, query_rows)
        key_frames = lax.dynamic_slice_in_dim(frame_ids, key_start, key_span)
        key_index = key_start + jnp.arange(key_span, dtype=jnp.int32)
        key_video = (key_index >= FIRST_TOK).astype(jnp.int32)
        allowed = (key_video == query_video)[None, :] & (key_frames[None, :] <= query_frames[:, None])
        scores = jnp.einsum('tgpd,ngd->gptn', block_queries, video_keys) * score_scale
        screened = jnp.where(allowed, scores, -1e+30)
        top_score = lax.optimization_barrier(jnp.max(screened, axis=-1))
        weights = jnp.where(allowed, jnp.exp(screened - top_score[..., None]), 0.0)
        denominator = lax.optimization_barrier(jnp.sum(weights, axis=-1))
        rounded = lax.optimization_barrier(weights.astype(jnp.bfloat16)).astype(jnp.float32)
        mixed = jnp.einsum('gptn,ngd->gptd', rounded, video_values) / denominator[..., None]
        return mixed.transpose(2, 0, 1, 3).reshape(query_rows, KVH * QPK * HD).astype(jnp.bfloat16)
    attended = lax.map(attend_block, jnp.arange(TOKENS // query_rows, dtype=jnp.int32))
    return attended.reshape(TOKENS, KVH * QPK * HD)
```

```python
import math

import jax
import jax.numpy as jnp
from jax import lax
from jax.experimental import pallas as pl
from jax.experimental.pallas import tpu as pltpu
from jax.sharding import PartitionSpec as P

HD = 128
QPK = 4
TOK = 128
QUARTER = 32
HALF = 16
HID = 4096
NY, NZ, NX, NC = 8, 3, 4, 2
FIRST_NY = 5
FAR = 4
NEG = -1e30
LOG2E = 1.0 / math.log(2.0)


def split_index(i):
    return i // (NZ * NX * NC), i // (NX * NC) % NZ, i // NC % NX, i % NC


def join_index(y, z, x, c):
    return ((y * NZ + z) * NX + x) * NC + c


def move(shard, target):
    pairs = []
    for i in range(NY * NZ * NX * NC):
        to = target(*split_index(i))
        if to is not None:
            pairs.append((i, join_index(*to)))
    return lax.ppermute(shard, "ctx", pairs)


def along_y(shard, by):
    def target(y, z, x, c):
        to = y + by
        if to >= NY or (to >= FIRST_NY) != (y >= FIRST_NY):
            return None
        return to, z, x, c

    return move(shard, target)


def along_z(shard, by):
    return move(shard, lambda y, z, x, c: (y, (z + by) % NZ, x, c))


def along_x(shard, by):
    return move(shard, lambda y, z, x, c: (y, z, (x + by) % NX, c))


def other_core(shard):
    return move(shard, lambda y, z, x, c: (y, z, x, 1 - c))


def next_slab(shard):
    count = NY * NZ * NX * NC
    first = FIRST_NY * NZ * NX * NC
    return lax.ppermute(shard, "ctx", [(i, i + 1) for i in range(count - 1) if i + 1 != first])


def along_head(shard, by):
    return lax.ppermute(shard, "head", [(i, (i + by) % 4) for i in range(4)])


def rows_of(q):
    return jnp.concatenate([q[:, p * HD : (p + 1) * HD] for p in range(QPK)], axis=0)


def scores_of(q, keys):
    return lax.dot_general(q, keys, (((1,), (1,)), ((), ())), preferred_element_type=jnp.float32)


def with_ones(values):
    return jnp.concatenate([values, jnp.ones(values.shape, values.dtype)], axis=1)


def near_kernel(q_ref, own_ref, other_ref, qf_ref, kf_ref, bias_ref, acc_ref, top_ref):
    q = rows_of(q_ref[0])
    diag = jnp.concatenate([own_ref[0:TOK, :], other_ref[0:TOK, :]], axis=0)
    s0 = scores_of(q, diag[:, :HD])
    s0 = jnp.where(kf_ref[...] <= qf_ref[...], s0, NEG)
    s1 = scores_of(q, own_ref[TOK:, :HD]) + bias_ref[...]
    s2 = scores_of(q, other_ref[TOK:, :HD]) + bias_ref[...]
    top = jnp.maximum(
        jnp.max(s0, axis=1, keepdims=True),
        jnp.maximum(jnp.max(s1, axis=1, keepdims=True), jnp.max(s2, axis=1, keepdims=True)),
    )
    acc = jnp.zeros((q.shape[0], 2 * HD), jnp.float32)
    for s, v in (
        (s0, diag[:, HD:]),
        (s1, own_ref[TOK:, HD:]),
        (s2, other_ref[TOK:, HD:]),
    ):
        w = jnp.exp2(s - top).astype(jnp.bfloat16)
        acc += jnp.dot(w, with_ones(v), preferred_element_type=jnp.float32)
    acc_ref[...] = acc
    top_ref[...] = jnp.broadcast_to(top, top_ref.shape)


def far_kernel(q_ref, own_ref, other_ref, bias_ref, acc_in, top_in, out_ref):
    q = rows_of(q_ref[0])
    half = own_ref.shape[0] // 2
    parts = []
    top = top_in[:, 0:1]
    for ref in (own_ref, other_ref):
        for b in range(2):
            s = scores_of(q, ref[b * half : (b + 1) * half, :HD])
            s = s + bias_ref[:, b * half : (b + 1) * half]
            parts.append((s, ref[b * half : (b + 1) * half, HD:]))
            top = jnp.maximum(top, jnp.max(s, axis=1, keepdims=True))
    acc = acc_in[...] * jnp.exp2(top_in[:, 0:1] - top)
    for s, v in parts:
        w = jnp.exp2(s - top).astype(jnp.bfloat16)
        acc += jnp.dot(w, with_ones(v), preferred_element_type=jnp.float32)
    total = acc[:, HD:]
    out_ref[0, : QPK * TOK, :] = (acc[:, :HD] / total).astype(jnp.bfloat16)
    level = top + jnp.log2(total)
    eye = lax.broadcasted_iota(jnp.int32, (TOK, TOK), 0) == lax.broadcasted_iota(
        jnp.int32, (TOK, TOK), 1
    )
    rows = [
        jnp.sum(jnp.where(eye, level[p * TOK : (p + 1) * TOK], 0.0), axis=0, keepdims=True)
        for p in range(QPK)
    ]
    level = jnp.concatenate(rows, axis=0)
    high = level.astype(jnp.bfloat16)
    rest = level - high.astype(jnp.float32)
    mid = rest.astype(jnp.bfloat16)
    low = (rest - mid.astype(jnp.float32)).astype(jnp.bfloat16)
    zero = jnp.zeros_like(low)
    out_ref[0, QPK * TOK :, :] = jnp.concatenate([high, mid, low, zero], axis=0)


def join_kernel(head_ref, a_ref, b_ref, c_ref, d_ref, out_ref):
    head = head_ref[0]
    eye = lax.broadcasted_iota(jnp.int32, (TOK, TOK), 0) == lax.broadcasted_iota(
        jnp.int32, (TOK, TOK), 1
    )
    refs = (a_ref, b_ref, c_ref, d_ref)
    levels = []
    for ref in refs:
        tail = ref[0, QPK * TOK :, :].astype(jnp.float32)
        levels.append(tail[0:4] + tail[4:8] + tail[8:12])
    top = jnp.maximum(
        jnp.maximum(levels[0], levels[1]), jnp.maximum(levels[2], levels[3])
    )
    shares = [jnp.exp2(level - top) for level in levels]
    total = shares[0] + shares[1] + shares[2] + shares[3]
    shares = [share / total for share in shares]
    for p in range(QPK):
        mixed = jnp.zeros((TOK, HD), jnp.float32)
        for ref, share in zip(refs, shares):
            column = jnp.sum(
                jnp.where(eye, jnp.broadcast_to(share[p : p + 1], (TOK, TOK)), 0.0),
                axis=1,
                keepdims=True,
            )
            mixed += column * ref[0, p * TOK : (p + 1) * TOK, :].astype(jnp.float32)
        mixed = mixed.astype(jnp.bfloat16)
        for quarter in range(4):
            row = pl.multiple_of(lax.rem(quarter + head, 4) * QUARTER, QUARTER)
            out_ref[pl.ds(row, QUARTER), p * HD : (p + 1) * HD] = mixed[
                quarter * QUARTER : (quarter + 1) * QUARTER
            ]


def whole(shape):
    return pl.BlockSpec(shape, lambda i: (0,) * len(shape))


ROWS = QPK * TOK


def attend_near(q, own, other, qf, kf, bias):
    return pl.pallas_call(
        near_kernel,
        grid=(NX,),
        in_specs=[
            pl.BlockSpec((1, TOK, QPK * HD), lambda i: (i, 0, 0)),
            whole(own.shape),
            whole(other.shape),
            pl.BlockSpec((ROWS, 1), lambda i: (i, 0)),
            whole(kf.shape),
            whole(bias.shape),
        ],
        out_specs=[
            pl.BlockSpec((ROWS, 2 * HD), lambda i: (i, 0)),
            pl.BlockSpec((ROWS, HD), lambda i: (i, 0)),
        ],
        out_shape=[
            jax.ShapeDtypeStruct((NX * ROWS, 2 * HD), jnp.float32),
            jax.ShapeDtypeStruct((NX * ROWS, HD), jnp.float32),
        ],
        name="near",
    )(q, own, other, qf, kf, bias)


def attend_far(q, own, other, bias, acc, top):
    return pl.pallas_call(
        far_kernel,
        grid=(NX,),
        in_specs=[
            pl.BlockSpec((1, TOK, QPK * HD), lambda i: (i, 0, 0)),
            whole(own.shape),
            whole(other.shape),
            whole(bias.shape),
            pl.BlockSpec((ROWS, 2 * HD), lambda i: (i, 0)),
            pl.BlockSpec((ROWS, HD), lambda i: (i, 0)),
        ],
        out_specs=pl.BlockSpec((1, ROWS + 16, HD), lambda i: (i, 0, 0)),
        out_shape=jax.ShapeDtypeStruct((NX, ROWS + 16, HD), jnp.bfloat16),
        name="far",
    )(q, own, other, bias, acc, top)


def join(head, parts):
    spec = pl.BlockSpec((1, ROWS + 16, HD), lambda i, h: (0, 0, 0))
    return pl.pallas_call(
        join_kernel,
        grid_spec=pltpu.PrefetchScalarGridSpec(
            num_scalar_prefetch=1,
            grid=(1,),
            in_specs=[spec] * 4,
            out_specs=pl.BlockSpec((TOK, QPK * HD), lambda i, h: (0, 0)),
        ),
        out_shape=jax.ShapeDtypeStruct((TOK, QPK * HD), jnp.bfloat16),
        name="join",
    )(head, *parts)


def before(patches, merge_index, merge_vals, merger_weight, proj_weight, frame_ids):
    position = lax.axis_index("ctx")
    head = lax.axis_index("head")
    y, z, x, c = split_index(position)
    f32 = jnp.float32

    edge = next_slab(patches[TOK:])
    local = merge_index[0] - (2 * position - 1)
    lower = jnp.where(local[0] == 0, edge, patches[:TOK])
    upper = jnp.where(local[1] == 1, patches[:TOK], patches[TOK:])
    vals = jnp.roll(merge_vals[0], -QUARTER * head, axis=1)
    merged = jnp.dot(vals[0], lower, preferred_element_type=f32) + jnp.dot(
        vals[1], upper, preferred_element_type=f32
    )
    partial = jnp.dot(
        merged.astype(jnp.bfloat16), merger_weight, preferred_element_type=f32
    ).astype(jnp.bfloat16)

    def piece(q, b):
        start = q * QUARTER + b * HALF
        return partial[start : start + HALF]

    up = along_head(jnp.concatenate([piece(2, 0), piece(1, 1)], axis=0), 1)
    down = along_head(jnp.concatenate([piece(2, 1), piece(3, 0)], axis=0), -1)
    up2 = along_head((piece(1, 0).astype(f32) + up[:HALF]).astype(jnp.bfloat16), 1)
    down2 = along_head((piece(3, 1).astype(f32) + down[:HALF]).astype(jnp.bfloat16), -1)
    first = piece(0, 0).astype(f32) + up2 + down[HALF:]
    second = piece(0, 1).astype(f32) + down2 + up[HALF:]
    hidden = jnp.concatenate([first, second], axis=0)
    mean_square = jnp.mean(hidden * hidden, axis=-1, keepdims=True)
    normed = (hidden * lax.rsqrt(mean_square + 1e-06)).astype(jnp.bfloat16)
    below = along_head(normed, 1)
    above = along_head(normed, -1)
    across_a = along_head(above[:HALF], -1)
    across_b = along_head(below[HALF:], 1)
    normed = jnp.concatenate([normed, above, across_a, across_b, below], axis=0)

    keyvals = jnp.dot(normed, proj_weight[:, QPK * HD :], preferred_element_type=f32).astype(
        jnp.bfloat16
    )
    queries = jnp.dot(normed, proj_weight[:, : QPK * HD], preferred_element_type=f32)
    queries = (queries * (LOG2E / math.sqrt(HD))).astype(jnp.bfloat16)

    column = jnp.concatenate(
        [keyvals] + [along_y(keyvals, by) for by in range(1, FAR + 1)], axis=0
    )
    q_all = jnp.stack([queries] + [along_x(queries, by) for by in range(1, NX)], axis=0)
    column_other = other_core(column)
    sides = jnp.concatenate([along_z(column, 1), along_z(column, 2)], axis=0)
    sides_other = other_core(sides)

    def slab_frames(slab):
        frames = lax.dynamic_slice_in_dim(frame_ids, slab * TOK, TOK)
        return jnp.roll(frames, -QUARTER * head)

    kf = jnp.concatenate(
        [slab_frames(position), slab_frames(join_index(y, z, x, 1 - c))]
    ).reshape(1, 2 * TOK)
    qf = jnp.stack([slab_frames(join_index(y, z, (x - by) % NX, c)) for by in range(NX)])
    qf = jnp.broadcast_to(qf[:, None, :], (NX, QPK, TOK)).reshape(NX * ROWS, 1)
    earlier = jnp.where(y >= FIRST_NY, y - FIRST_NY, y)
    distance = jnp.arange(FAR + 1)
    bias_near = jnp.where(distance[1:] <= earlier, 0.0, NEG).astype(f32)
    bias_far = []
    for by in (1, 2):
        ok = (distance <= earlier) & ((distance > 0) | (z >= by))
        bias_far.append(jnp.where(ok, 0.0, NEG).astype(f32))
    bias_near = jnp.repeat(bias_near, TOK).reshape(1, -1)
    bias_far = jnp.repeat(jnp.concatenate(bias_far), TOK).reshape(1, -1)
    return q_all, column, column_other, sides, sides_other, qf, kf, bias_near, bias_far


def local_attention(q_all, column, column_other, sides, sides_other, qf, kf, bias_near, bias_far):
    acc, top = attend_near(q_all, column, column_other, qf, kf, bias_near)
    return attend_far(q_all, sides, sides_other, bias_far, acc, top)


def after(parts):
    head = lax.axis_index("head").reshape(1).astype(jnp.int32)
    pieces = [parts[0:1]] + [along_x(parts[by : by + 1], -by) for by in range(1, NX)]
    return join(head, pieces)


def body(patches, merge_index, merge_vals, merger_weight, proj_weight, frame_ids):
    operands = before(patches, merge_index, merge_vals, merger_weight, proj_weight, frame_ids)
    return after(local_attention(*operands))


def solution(mesh):
    return jax.shard_map(
        body,
        mesh=mesh,
        in_specs=(
            P("ctx", "head"),
            P("ctx", None),
            P("ctx", None, None, None),
            P("head", None),
            P(None, "head"),
            P(),
        ),
        out_specs=P("ctx", "head"),
        check_vma=False,
    )
```

```python
import math

import jax
import jax.numpy as jnp
from jax import lax
from jax.experimental import pallas as pl
from jax.experimental.pallas import tpu as pltpu
from jax.sharding import PartitionSpec as P


HD = 128
QPK = 4
TOK = 128
QUARTER = 32
HALF = 16
NY, NZ, NX, NC = 8, 3, 4, 2
FIRST_NY = 5
FAR = 4
NEG = -1e30
LOG2E = 1.0 / math.log(2.0)


def split_index(i):
    return i // (NZ * NX * NC), i // (NX * NC) % NZ, i // NC % NX, i % NC


def join_index(y, z, x, c):
    return ((y * NZ + z) * NX + x) * NC + c


def move(shard, target):
    pairs = []
    for i in range(NY * NZ * NX * NC):
        to = target(*split_index(i))
        if to is not None:
            pairs.append((i, join_index(*to)))
    return lax.ppermute(shard, "ctx", pairs)


def along_y(shard, by):
    def target(y, z, x, c):
        to = y + by
        if to >= NY or (to >= FIRST_NY) != (y >= FIRST_NY):
            return None
        return to, z, x, c

    return move(shard, target)


def along_z(shard, by):
    return move(shard, lambda y, z, x, c: (y, (z + by) % NZ, x, c))


def along_x(shard, by):
    return move(shard, lambda y, z, x, c: (y, z, (x + by) % NX, c))


def other_core(shard):
    return move(shard, lambda y, z, x, c: (y, z, x, 1 - c))


def next_slab(shard):
    count = NY * NZ * NX * NC
    first = FIRST_NY * NZ * NX * NC
    return lax.ppermute(shard, "ctx", [(i, i + 1) for i in range(count - 1) if i + 1 != first])


def along_head(shard, by):
    return lax.ppermute(shard, "head", [(i, (i + by) % 4) for i in range(4)])


def rows_of(q):
    return jnp.concatenate([q[:, p * HD : (p + 1) * HD] for p in range(QPK)], axis=0)


def scores_of(q, keys):
    return lax.dot_general(q, keys, (((1,), (1,)), ((), ())), preferred_element_type=jnp.float32)


def with_ones(values):
    return jnp.concatenate([values, jnp.ones(values.shape, values.dtype)], axis=1)


def eye():
    shape = (TOK, TOK)
    return lax.broadcasted_iota(jnp.int32, shape, 0) == lax.broadcasted_iota(jnp.int32, shape, 1)


def as_column(row):
    square = jnp.where(eye(), jnp.broadcast_to(row, (TOK, TOK)), 0.0)
    return jnp.sum(square, axis=1, keepdims=True)


def as_row(square):
    return jnp.sum(jnp.where(eye(), square, 0.0), axis=0, keepdims=True)


def saved(acc, top):
    lane = lax.broadcasted_iota(jnp.int32, (1, HD), 1)
    return jnp.concatenate([acc[:, :HD], jnp.where(lane < HD // 2, acc[:, HD:], top)], axis=1)


def restored(state_ref):
    total = jnp.broadcast_to(state_ref[:, HD : HD + 1], (state_ref.shape[0], HD))
    return jnp.concatenate([state_ref[:, :HD], total], axis=1), state_ref[:, 2 * HD - 1 : 2 * HD]


def weighted(parts, top, acc):
    for s, v in parts:
        w = jnp.exp2(s - top).astype(jnp.bfloat16)
        acc += jnp.dot(w, with_ones(v), preferred_element_type=jnp.float32)
    return acc


def near_kernel(place_ref, q_ref, own_ref, other_ref, frames_ref, state_ref):
    earlier, x, c = place_ref[0], place_ref[2], place_ref[3]
    q = rows_of(q_ref[0])
    mine = frames_ref[pl.ds(lax.rem(x + NX - pl.program_id(0), NX) * NC + c, 1), :]
    column = as_column(mine.astype(jnp.float32))
    column = jnp.concatenate([column] * QPK, axis=0)
    parts = []
    for ref, row in ((own_ref, x * NC + c), (other_ref, x * NC + 1 - c)):
        frame = frames_ref[pl.ds(row, 1), :].astype(jnp.float32)
        s = scores_of(q, ref[:TOK, :HD])
        parts.append((jnp.where(frame <= column, s, NEG), ref[:TOK, HD:]))
    lane = lax.broadcasted_iota(jnp.int32, (1, FAR * TOK), 1)
    bias = jnp.where(lane < earlier * TOK, 0.0, NEG)
    for ref in (own_ref, other_ref):
        parts.append((scores_of(q, ref[TOK:, :HD]) + bias, ref[TOK:, HD:]))
    top = jnp.full((ROWS, 1), NEG, jnp.float32)
    for s, _ in parts:
        top = jnp.maximum(top, jnp.max(s, axis=1, keepdims=True))
    acc = weighted(parts, top, jnp.zeros((ROWS, 2 * HD), jnp.float32))
    state_ref[...] = saved(acc, top)


def far_sum(place_ref, q_ref, sides_ref, state_ref):
    earlier, z = place_ref[0], place_ref[1]
    q = rows_of(q_ref[0])
    half = (FAR + 1) * TOK
    acc, old = restored(state_ref)
    lane = lax.broadcasted_iota(jnp.int32, (1, half), 1)
    parts = []
    top = old
    for b in range(2):
        low = jnp.where(z >= b + 1, 0, TOK)
        bias = jnp.where((lane >= low) & (lane < (earlier + 1) * TOK), 0.0, NEG)
        s = scores_of(q, sides_ref[b * half : (b + 1) * half, :HD]) + bias
        parts.append((s, sides_ref[b * half : (b + 1) * half, HD:]))
        top = jnp.maximum(top, jnp.max(s, axis=1, keepdims=True))
    return weighted(parts, top, acc * jnp.exp2(old - top)), top


def mid_kernel(place_ref, q_ref, sides_ref, state_in, state_ref):
    acc, top = far_sum(place_ref, q_ref, sides_ref, state_in)
    state_ref[...] = saved(acc, top)


def last_kernel(place_ref, q_ref, sides_ref, state_in, out_ref):
    acc, top = far_sum(place_ref, q_ref, sides_ref, state_in)
    total = acc[:, HD:]
    out_ref[: QPK * TOK, :] = (acc[:, :HD] / total).astype(jnp.bfloat16)
    level = top + jnp.log2(total)
    level = jnp.concatenate(
        [as_row(level[p * TOK : (p + 1) * TOK]) for p in range(QPK)], axis=0
    )
    high = level.astype(jnp.bfloat16)
    rest = level - high.astype(jnp.float32)
    mid = rest.astype(jnp.bfloat16)
    low = (rest - mid.astype(jnp.float32)).astype(jnp.bfloat16)
    zero = jnp.zeros_like(low)
    out_ref[QPK * TOK :, :] = jnp.concatenate([high, mid, low, zero], axis=0)


def join_kernel(place_ref, a_ref, b_ref, c_ref, d_ref, out_ref):
    head = place_ref[4]
    refs = (a_ref, b_ref, c_ref, d_ref)
    levels = []
    for ref in refs:
        tail = ref[QPK * TOK :, :].astype(jnp.float32)
        levels.append(tail[0:4] + tail[4:8] + tail[8:12])
    top = jnp.maximum(
        jnp.maximum(levels[0], levels[1]), jnp.maximum(levels[2], levels[3])
    )
    shares = [jnp.exp2(level - top) for level in levels]
    total = shares[0] + shares[1] + shares[2] + shares[3]
    shares = [share / total for share in shares]
    for p in range(QPK):
        mixed = jnp.zeros((TOK, HD), jnp.float32)
        for ref, share in zip(refs, shares):
            part = ref[p * TOK : (p + 1) * TOK, :].astype(jnp.float32)
            mixed += as_column(share[p : p + 1]) * part
        mixed = mixed.astype(jnp.bfloat16)
        for quarter in range(4):
            row = pl.multiple_of(lax.rem(quarter + head, 4) * QUARTER, QUARTER)
            out_ref[pl.ds(row, QUARTER), p * HD : (p + 1) * HD] = mixed[
                quarter * QUARTER : (quarter + 1) * QUARTER
            ]


ROWS = QPK * TOK


def whole(a):
    return pl.BlockSpec(a.shape, lambda i, place: (0,) * a.ndim)


def local_call(kernel, steps, in_specs, out_spec, out_shape, operands):
    return pl.pallas_call(
        kernel,
        grid_spec=pltpu.PrefetchScalarGridSpec(
            num_scalar_prefetch=1, grid=(steps,), in_specs=in_specs, out_specs=out_spec
        ),
        out_shape=out_shape,
    )(*operands)


STATE = jax.ShapeDtypeStruct((NX * ROWS, 2 * HD), jnp.float32)


def attend_near(place, q, own, other, frames):
    return local_call(
        near_kernel,
        NX,
        [
            pl.BlockSpec((1, TOK, QPK * HD), lambda i, place: (i, 0, 0)),
            whole(own),
            whole(other),
            whole(frames),
        ],
        pl.BlockSpec((ROWS, 2 * HD), lambda i, place: (i, 0)),
        STATE,
        (place, q, own, other, frames),
    )


def attend_mid(place, q, sides, state):
    return local_call(
        mid_kernel,
        NX,
        [
            pl.BlockSpec((1, TOK, QPK * HD), lambda i, place: (i, 0, 0)),
            whole(sides),
            pl.BlockSpec((ROWS, 2 * HD), lambda i, place: (i, 0)),
        ],
        pl.BlockSpec((ROWS, 2 * HD), lambda i, place: (i, 0)),
        STATE,
        (place, q, sides, state),
    )


def attend_last(place, q, sides, state, slab):
    return local_call(
        last_kernel,
        1,
        [
            pl.BlockSpec((1, TOK, QPK * HD), lambda i, place: (slab, 0, 0)),
            whole(sides),
            pl.BlockSpec((ROWS, 2 * HD), lambda i, place: (slab, 0)),
        ],
        pl.BlockSpec((ROWS + 16, HD), lambda i, place: (0, 0)),
        jax.ShapeDtypeStruct((ROWS + 16, HD), jnp.bfloat16),
        (place, q, sides, state),
    )


def join(place, parts):
    return local_call(
        join_kernel,
        1,
        [whole(part) for part in parts],
        pl.BlockSpec((TOK, QPK * HD), lambda i, place: (0, 0)),
        jax.ShapeDtypeStruct((TOK, QPK * HD), jnp.bfloat16),
        (place, *parts),
    )


def body(patches, merge_index, merge_vals, merger_weight, proj_weight, frame_ids):
    position = lax.axis_index("ctx")
    head = lax.axis_index("head")
    y, z, x, c = split_index(position)
    f32 = jnp.float32

    earlier = jnp.where(y >= FIRST_NY, y - FIRST_NY, y)
    place = jnp.stack([earlier, z, x, c, head]).astype(jnp.int32)
    edge = next_slab(patches[TOK:])
    local = merge_index[0] - (2 * position - 1)
    lower = jnp.where(local[0] == 0, edge, patches[:TOK])
    upper = jnp.where(local[1] == 1, patches[:TOK], patches[TOK:])
    vals = jnp.roll(merge_vals[0], -QUARTER * head, axis=1)
    merged = jnp.dot(vals[0], lower, preferred_element_type=f32) + jnp.dot(
        vals[1], upper, preferred_element_type=f32
    )
    partial = jnp.dot(
        merged.astype(jnp.bfloat16), merger_weight, preferred_element_type=f32
    ).astype(jnp.bfloat16)

    def piece(q, b):
        start = q * QUARTER + b * HALF
        return partial[start : start + HALF]

    up = along_head(jnp.concatenate([piece(2, 0), piece(1, 1)], axis=0), 1)
    down = along_head(jnp.concatenate([piece(2, 1), piece(3, 0)], axis=0), -1)
    up2 = along_head((piece(1, 0).astype(f32) + up[:HALF]).astype(jnp.bfloat16), 1)
    down2 = along_head((piece(3, 1).astype(f32) + down[:HALF]).astype(jnp.bfloat16), -1)
    group = position // (NX * NC)
    octet = lax.dynamic_slice_in_dim(frame_ids, group * (NX * NC * TOK), NX * NC * TOK)
    octet = jnp.roll(octet.reshape(NX * NC, TOK), -QUARTER * head, axis=1)
    octet, place, up2 = lax.optimization_barrier((octet, place, up2))
    first = piece(0, 0).astype(f32) + up2 + down[HALF:]
    second = piece(0, 1).astype(f32) + down2 + up[HALF:]
    hidden = jnp.concatenate([first, second], axis=0)
    mean_square = jnp.mean(hidden * hidden, axis=-1, keepdims=True)
    normed = (hidden * lax.rsqrt(mean_square + 1e-06)).astype(jnp.bfloat16)
    below = along_head(normed, 1)
    above = along_head(normed, -1)
    across_a = along_head(above[:HALF], -1)
    across_b = along_head(below[HALF:], 1)
    normed = jnp.concatenate([normed, above, across_a, across_b, below], axis=0)

    keyvals = jnp.dot(normed, proj_weight[:, QPK * HD :], preferred_element_type=f32)
    keyvals = keyvals.astype(jnp.bfloat16)
    queries = jnp.dot(normed, proj_weight[:, : QPK * HD], preferred_element_type=f32)
    queries = (queries * (LOG2E / math.sqrt(HD))).astype(jnp.bfloat16)

    column = [keyvals]
    for by in range(1, FAR + 1):
        column.append(along_y(keyvals, by))
    column = jnp.concatenate(column, axis=0)
    q_all = [queries]
    for by in range(1, NX):
        q_all.append(along_x(queries, by))
    q_all = jnp.stack(q_all, axis=0)
    column_other = other_core(column)
    sides = []
    for by in (1, 2):
        sides.append(along_z(column, by))
    sides = jnp.concatenate(sides, axis=0)
    sides_other = other_core(sides)

    state = attend_near(place, q_all, column, column_other, octet)
    state = attend_mid(place, q_all, sides, state)
    parts = {}
    for by in (2, 1, 3, 0):
        part = attend_last(place, q_all, sides_other, state, by)
        if by:
            part = along_x(part, -by)
        parts[by] = part
    return join(place, [parts[by] for by in range(NX)])


def solution(mesh):
    return jax.shard_map(
        body,
        mesh=mesh,
        in_specs=(
            P("ctx", "head"),
            P("ctx", None),
            P("ctx", None, None, None),
            P("head", None),
            P(None, "head"),
            P(),
        ),
        out_specs=P("ctx", "head"),
        check_vma=False,
    )
```

```python
import functools
import math

import jax
import jax.numpy as jnp
from jax import lax
from jax.experimental import pallas as pl
from jax.experimental.pallas import tpu as pltpu
from jax.sharding import PartitionSpec as P


HD = 128
QPK = 4
TOK = 128
QUARTER = 32
HALF = 16
NY, NZ, NX, NC = 8, 3, 4, 2
FIRST_NY = 5
FAR = 4
NEG = -1e30
LOG2E = 1.0 / math.log(2.0)


def split_index(i):
    return i // (NZ * NX * NC), i // (NX * NC) % NZ, i // NC % NX, i % NC


def join_index(y, z, x, c):
    return ((y * NZ + z) * NX + x) * NC + c


def move(shard, target):
    pairs = []
    for i in range(NY * NZ * NX * NC):
        to = target(*split_index(i))
        if to is not None:
            pairs.append((i, join_index(*to)))
    return lax.ppermute(shard, "ctx", pairs)


def along_y(shard, by):
    def target(y, z, x, c):
        to = y + by
        if to >= NY or (to >= FIRST_NY) != (y >= FIRST_NY):
            return None
        return to, z, x, c

    return move(shard, target)


def along_z(shard, by):
    return move(shard, lambda y, z, x, c: (y, (z + by) % NZ, x, c))


def along_x(shard, by):
    return move(shard, lambda y, z, x, c: (y, z, (x + by) % NX, c))


def other_core(shard):
    return move(shard, lambda y, z, x, c: (y, z, x, 1 - c))


def next_slab(shard):
    count = NY * NZ * NX * NC
    first = FIRST_NY * NZ * NX * NC
    return lax.ppermute(shard, "ctx", [(i, i + 1) for i in range(count - 1) if i + 1 != first])


def along_head(shard, by):
    return lax.ppermute(shard, "head", [(i, (i + by) % 4) for i in range(4)])


def scores_of(q, keys):
    return lax.dot_general(q, keys, (((1,), (1,)), ((), ())), preferred_element_type=jnp.float32)


def with_ones(values):
    return jnp.concatenate([values, jnp.ones(values.shape, values.dtype)], axis=1)


def eye():
    shape = (TOK, TOK)
    return lax.broadcasted_iota(jnp.int32, shape, 0) == lax.broadcasted_iota(jnp.int32, shape, 1)


def as_column(row):
    square = jnp.where(eye(), jnp.broadcast_to(row, (TOK, TOK)), 0.0)
    return jnp.sum(square, axis=1, keepdims=True)


def as_row(square):
    return jnp.sum(jnp.where(eye(), square, 0.0), axis=0, keepdims=True)


def saved(acc, top):
    lane = lax.broadcasted_iota(jnp.int32, (1, HD), 1)
    return jnp.concatenate([acc[:, :HD], jnp.where(lane < HD // 2, acc[:, HD:], top)], axis=1)


def restored(state):
    total = jnp.broadcast_to(state[:, HD : HD + 1], (state.shape[0], HD))
    return jnp.concatenate([state[:, :HD], total], axis=1), state[:, 2 * HD - 1 :]


def flash(q, blocks, states):
    values = [with_ones(v) for _, v, _ in blocks]

    def scores(p):
        rows = q[:, p * HD : (p + 1) * HD]
        return [mask(scores_of(rows, keys)) for keys, _, mask in blocks]

    done = []
    following = scores(0)
    for p in range(QPK):
        current = following
        if p + 1 < QPK:
            following = scores(p + 1)
        top = jnp.full((TOK, 1), NEG, jnp.float32) if states is None else states[p][1]
        for s in current:
            top = jnp.maximum(top, jnp.max(s, axis=1, keepdims=True))
        acc = None if states is None else states[p][0] * jnp.exp2(states[p][1] - top)
        for s, v in zip(current, values):
            w = jnp.exp2(s - top).astype(jnp.bfloat16)
            part = jnp.dot(w, v, preferred_element_type=jnp.float32)
            acc = part if acc is None else acc + part
        done.append((acc, top))
    return done


def near_kernel(place_ref, q_ref, own_ref, other_ref, frames_ref, state_ref):
    earlier, x, c = place_ref[0], place_ref[2], place_ref[3]
    mine = frames_ref[pl.ds(lax.rem(x + NX - pl.program_id(0), NX) * NC + c, 1), :]
    column = as_column(mine.astype(jnp.float32))
    lane = lax.broadcasted_iota(jnp.int32, (1, FAR * TOK), 1)
    bias = jnp.where(lane < earlier * TOK, 0.0, NEG)
    blocks = []
    for ref, row in ((own_ref, x * NC + c), (other_ref, x * NC + 1 - c)):
        frame = frames_ref[pl.ds(row, 1), :].astype(jnp.float32)
        allowed = frame <= column
        blocks.append(
            (ref[:TOK, :HD], ref[:TOK, HD:], lambda s, ok=allowed: jnp.where(ok, s, NEG))
        )
        blocks.append((ref[TOK:, :HD], ref[TOK:, HD:], lambda s: s + bias))
    for p, (acc, top) in enumerate(flash(q_ref[0], blocks, None)):
        state_ref[p * TOK : (p + 1) * TOK, :] = saved(acc, top)


def far_kernel(place_ref, q_ref, own_ref, other_ref, state_ref, *out_refs):
    earlier, z = place_ref[0], place_ref[1]
    half = (FAR + 1) * TOK
    lane = lax.broadcasted_iota(jnp.int32, (1, half), 1)
    blocks = []
    for b in range(2):
        low = jnp.where(z >= b + 1, 0, TOK)
        bias = jnp.where((lane >= low) & (lane < (earlier + 1) * TOK), 0.0, NEG)
        for ref in (own_ref, other_ref):
            rows = slice(b * half, (b + 1) * half)
            blocks.append((ref[rows, :HD], ref[rows, HD:], lambda s, e=bias: s + e))
    states = [restored(state_ref[p * TOK : (p + 1) * TOK, :]) for p in range(QPK)]
    levels, pieces = [], []
    for acc, top in flash(q_ref[0], blocks, states):
        total = acc[:, HD:]
        pieces.append((acc[:, :HD] / total).astype(jnp.bfloat16))
        levels.append(as_row(top + jnp.log2(total)))
    level = jnp.concatenate(levels, axis=0)
    high = level.astype(jnp.bfloat16)
    rest = level - high.astype(jnp.float32)
    mid = rest.astype(jnp.bfloat16)
    low = (rest - mid.astype(jnp.float32)).astype(jnp.bfloat16)
    zero = jnp.zeros_like(low)
    pieces.append(jnp.concatenate([high, mid, low, zero], axis=0))

    def store(out_ref):
        for p, piece in enumerate(pieces):
            out_ref[p * TOK : p * TOK + piece.shape[0], :] = piece

    if len(out_refs) == 1:
        store(out_refs[0])
    else:
        for step, out_ref in enumerate(out_refs):
            pl.when(pl.program_id(0) == step)(functools.partial(store, out_ref))


def join_kernel(place_ref, a_ref, b_ref, c_ref, d_ref, out_ref):
    head = place_ref[4]
    refs = (a_ref, b_ref, c_ref, d_ref)
    levels = []
    for ref in refs:
        tail = ref[QPK * TOK :, :].astype(jnp.float32)
        levels.append(tail[0:4] + tail[4:8] + tail[8:12])
    top = jnp.maximum(
        jnp.maximum(levels[0], levels[1]), jnp.maximum(levels[2], levels[3])
    )
    shares = [jnp.exp2(level - top) for level in levels]
    total = shares[0] + shares[1] + shares[2] + shares[3]
    shares = [share / total for share in shares]
    for p in range(QPK):
        mixed = jnp.zeros((TOK, HD), jnp.float32)
        for ref, share in zip(refs, shares):
            part = ref[p * TOK : (p + 1) * TOK, :].astype(jnp.float32)
            mixed += as_column(share[p : p + 1]) * part
        mixed = mixed.astype(jnp.bfloat16)
        for quarter in range(4):
            row = pl.multiple_of(lax.rem(quarter + head, 4) * QUARTER, QUARTER)
            out_ref[pl.ds(row, QUARTER), p * HD : (p + 1) * HD] = mixed[
                quarter * QUARTER : (quarter + 1) * QUARTER
            ]


ROWS = QPK * TOK


def whole(a):
    return pl.BlockSpec(a.shape, lambda i, place: (0,) * a.ndim)


def local_call(kernel, steps, in_specs, out_spec, out_shape, operands):
    return pl.pallas_call(
        kernel,
        grid_spec=pltpu.PrefetchScalarGridSpec(
            num_scalar_prefetch=1, grid=(steps,), in_specs=in_specs, out_specs=out_spec
        ),
        out_shape=out_shape,
    )(*operands)


STATE = jax.ShapeDtypeStruct((NX * ROWS, 2 * HD), jnp.float32)


def attend_near(place, q, own, other, frames):
    return local_call(
        near_kernel,
        NX,
        [
            pl.BlockSpec((1, TOK, QPK * HD), lambda i, place: (i, 0, 0)),
            whole(own),
            whole(other),
            whole(frames),
        ],
        pl.BlockSpec((ROWS, 2 * HD), lambda i, place: (i, 0)),
        STATE,
        (place, q, own, other, frames),
    )


def attend_far(place, q, own, other, state, first, steps):
    part = jax.ShapeDtypeStruct((ROWS + 16, HD), jnp.bfloat16)
    return local_call(
        far_kernel,
        steps,
        [
            pl.BlockSpec((1, TOK, QPK * HD), lambda i, place: (first + i, 0, 0)),
            whole(own),
            whole(other),
            pl.BlockSpec((ROWS, 2 * HD), lambda i, place: (first + i, 0)),
        ],
        [whole(part)] * steps,
        [part] * steps,
        (place, q, own, other, state),
    )


def join(place, parts):
    return local_call(
        join_kernel,
        1,
        [whole(part) for part in parts],
        pl.BlockSpec((TOK, QPK * HD), lambda i, place: (0, 0)),
        jax.ShapeDtypeStruct((TOK, QPK * HD), jnp.bfloat16),
        (place, *parts),
    )


def body(patches, merge_index, merge_vals, merger_weight, proj_weight, frame_ids):
    position = lax.axis_index("ctx")
    head = lax.axis_index("head")
    y, z, x, c = split_index(position)
    f32 = jnp.float32

    earlier = jnp.where(y >= FIRST_NY, y - FIRST_NY, y)
    place = jnp.stack([earlier, z, x, c, head]).astype(jnp.int32)
    edge = next_slab(patches[TOK:])
    local = merge_index[0] - (2 * position - 1)
    lower = jnp.where(local[0] == 0, edge, patches[:TOK])
    upper = jnp.where(local[1] == 1, patches[:TOK], patches[TOK:])
    vals = jnp.roll(merge_vals[0], -QUARTER * head, axis=1)
    merged = jnp.dot(vals[0], lower, preferred_element_type=f32) + jnp.dot(
        vals[1], upper, preferred_element_type=f32
    )
    partial = jnp.dot(
        merged.astype(jnp.bfloat16), merger_weight, preferred_element_type=f32
    ).astype(jnp.bfloat16)

    def piece(q, b):
        start = q * QUARTER + b * HALF
        return partial[start : start + HALF]

    up_far = along_head(piece(2, 0), 1)
    down_far = along_head(piece(2, 1), -1)
    up_near = along_head(piece(1, 1), 1)
    down_near = along_head(piece(3, 0), -1)
    up2 = (piece(1, 0).astype(f32) + up_far).astype(jnp.bfloat16)
    up2 = along_head(up2, 1)
    down2 = (piece(3, 1).astype(f32) + down_far).astype(jnp.bfloat16)
    down2 = along_head(down2, -1)
    group = position // (NX * NC)
    octet = lax.dynamic_slice_in_dim(frame_ids, group * (NX * NC * TOK), NX * NC * TOK)
    octet = jnp.roll(octet.reshape(NX * NC, TOK), -QUARTER * head, axis=1)
    octet, place, up2, down2, up_near, down_near = lax.optimization_barrier(
        (octet, place, up2, down2, up_near, down_near)
    )
    first = piece(0, 0).astype(f32) + up2 + down_near
    second = piece(0, 1).astype(f32) + down2 + up_near
    hidden = jnp.concatenate([first, second], axis=0)
    mean_square = jnp.mean(hidden * hidden, axis=-1, keepdims=True)
    normed = (hidden * lax.rsqrt(mean_square + 1e-06)).astype(jnp.bfloat16)
    early, late = normed[:HALF], normed[HALF:]
    above_early = along_head(early, -1)
    below_late = along_head(late, 1)
    above_late = along_head(late, -1)
    below_early = along_head(early, 1)
    across_early = along_head(above_early, -1)
    across_late = along_head(below_late, 1)
    normed = jnp.concatenate(
        [normed, above_early, above_late, across_early, across_late, below_early, below_late],
        axis=0,
    )

    keyvals = jnp.dot(normed, proj_weight[:, QPK * HD :], preferred_element_type=f32)
    keyvals = keyvals.astype(jnp.bfloat16)
    queries = jnp.dot(normed, proj_weight[:, : QPK * HD], preferred_element_type=f32)
    queries = (queries * (LOG2E / math.sqrt(HD))).astype(jnp.bfloat16)

    column = [keyvals]
    for by in range(1, FAR + 1):
        column.append(along_y(keyvals, by))
    column = jnp.concatenate(column, axis=0)
    q_all = [queries]
    for by in range(1, NX):
        q_all.append(along_x(queries, by))
    q_all = jnp.stack(q_all, axis=0)
    column_other = other_core(column)
    sides = []
    for by in (1, 2):
        sides.append(along_z(column, by))
    sides = jnp.concatenate(sides, axis=0)
    sides_other = other_core(sides)

    state = attend_near(place, q_all, column, column_other, octet)
    parts = {}
    for first, steps in ((1, 3), (0, 1)):
        made = attend_far(place, q_all, sides, sides_other, state, first, steps)
        for by, part in enumerate(made, first):
            if by:
                part = along_x(part, -by)
            parts[by] = part
    return join(place, [parts[by] for by in range(NX)])


def solution(mesh):
    return jax.shard_map(
        body,
        mesh=mesh,
        in_specs=(
            P("ctx", "head"),
            P("ctx", None),
            P("ctx", None, None, None),
            P("head", None),
            P(None, "head"),
            P(),
        ),
        out_specs=P("ctx", "head"),
        check_vma=False,
    )
```
